32 devices in a mesh: shot: 16 (over z, y, core), rec: 2 (over x).
Axes of the slice: x: 2, y: 2, z: 4, core: 2. Of those that a mesh axis runs over, the one named last changes fastest.
Arguments:
- survey: float32 [2, 8, 2048, 2048], P(None, None, 'shot', 'rec'), may hold values from -1.5 to 1.5
- panel_index: int32 [2], replicated, may hold values from 0 to 31
Outputs:
- predicted: float32 [64, 2048, 2048], P(None, 'shot', 'rec')
The draws below stay inside these ranges and needn't reach their ends.
Inputs may be any that keep to these rules, and one draw needn't show every extreme that they name: `panel_index`: panel numbers; one panel may come twice.
All inputs are finite; a program needn't handle non-finite values.
Results may differ from the reference program's by a relative error of at most 0.0001.
Values sent between devices are 32-bit elements; how exact they have to be, the bound alone decides.
A program may use at most 192 MiB of HBM per device.

```python
import math
import jax
import jax.numpy as jnp
from jax import lax

ORDER = 2048
FREQS = 8
FIRST_BIN = 8
TRACE_LEN = 400
SAMPLES = 64
PANEL = 64
STEPS = 2


def steps_of(own_key, extent, split, least, high):
    level = 1.0
    for axis_at, shards_of in split:
        heights = jax.random.uniform(jax.random.fold_in(jax.random.fold_in(own_key, 6), axis_at), (shards_of,), jnp.float32, least / len(split), high / len(split))
        level = level * jnp.repeat(jnp.exp(heights), extent[axis_at] // shards_of).reshape((-1,) + (1,) * (len(extent) - 1 - axis_at))
    return level


def gaussian(own_key, extent, width, limit, split=(), kind=jnp.bfloat16):
    loudness = steps_of(own_key, extent, split, -0.22, 0.18) if split else 1.0
    entries = jax.random.normal(own_key, extent, jnp.float32) * width * loudness
    return jnp.minimum(jnp.maximum(entries, -limit), limit).astype(kind)


def setup_inputs(seed: int = 0) -> dict:
    arg_keys = jax.random.split(jax.random.key(seed), 3)
    survey = gaussian(arg_keys[0], (2, FREQS, ORDER, ORDER), 0.25, 1.5, ((2, 16), (3, 2)), jnp.float32)
    panel_index = jax.random.randint(arg_keys[1], (STEPS,), 0, ORDER // PANEL).astype(jnp.int32)
    return dict(survey=survey, panel_index=panel_index)


def build_tables(nfreq):
    bins = jnp.arange(nfreq, dtype=jnp.int32) + FIRST_BIN
    moments = jnp.arange(SAMPLES, dtype=jnp.int32)
    phase = moments[:, None] * bins[None, :] % TRACE_LEN
    angle = phase.astype(jnp.float32) * (2.0 * math.pi / TRACE_LEN)
    factor = 1.0 / math.sqrt(nfreq)
    return (jnp.cos(angle) * factor, jnp.sin(angle) * factor)

def multiply(left_operand, right_operand):
    return jnp.einsum('vdb,vbg->vdg', left_operand, right_operand, precision=lax.Precision.HIGHEST, preferred_element_type=jnp.float32)

def reference(survey, panel_index):
    real_part = survey[0]
    imag_part = survey[1]
    cosine_lookup, sine_lookup = build_tables(FREQS)
    height = min(ORDER, 256)
    outputs = []
    for block_start in range(0, ORDER, height):
        running_real = jnp.zeros((FREQS, height, ORDER), jnp.float32)
        running_imaginary = jnp.zeros((FREQS, height, ORDER), jnp.float32)
        for index_step in range(STEPS):
            start = (panel_index[index_step] * PANEL).astype(jnp.int32)
            left_real = lax.dynamic_slice_in_dim(real_part[:, block_start:block_start + height], start, PANEL, 2)
            left_imag = lax.dynamic_slice_in_dim(imag_part[:, block_start:block_start + height], start, PANEL, 2)
            right_real = lax.dynamic_slice_in_dim(real_part, start, PANEL, 1)
            right_imag = lax.dynamic_slice_in_dim(imag_part, start, PANEL, 1)
            running_real = running_real + (multiply(left_real, right_real) - multiply(left_imag, right_imag))
            running_imaginary = running_imaginary + (multiply(left_real, right_imag) + multiply(left_imag, right_real))
        time_domain_output = jnp.einsum('ay,yjk->ajk', cosine_lookup, running_real, precision=lax.Precision.HIGHEST, preferred_element_type=jnp.float32)
        time_domain_output = time_domain_output - jnp.einsum('ay,yjk->ajk', sine_lookup, running_imaginary, precision=lax.Precision.HIGHEST, preferred_element_type=jnp.float32)
        outputs.append(time_domain_output)
    return jnp.concatenate(outputs, axis=1)
```

```python
import functools
import math

import jax
import jax.numpy as jnp
import numpy as np
from jax import lax
from jax.experimental import pallas as pl
from jax.experimental.pallas import tpu as pltpu
from jax.sharding import PartitionSpec as P

FIRST_BIN = 8
TRACE_LEN = 400
SAMPLES = 64
PANEL = 64
STEPS = 2
SLOTS = 3
WINDOW = 4
LAG = 2
AHEAD = 4


def from_root(array, axis, root):
    mine = lax.axis_index(axis) == root
    return lax.psum(jnp.where(mine, array, jnp.zeros_like(array)), axis)


def middle(f):
    angle = 2.0 * math.pi * (f + FIRST_BIN) * (0.5 * (SAMPLES - 1)) / TRACE_LEN
    return math.cos(angle), math.sin(angle)


def kron_tables(nfreq):
    moments = np.arange(SAMPLES // 2) + 0.5
    bins = np.arange(nfreq) + FIRST_BIN
    angle = moments[:, None] * bins[None, :] * (2.0 * math.pi / TRACE_LEN)
    parts = []
    for wave in (np.cos(angle), np.sin(angle)):
        flat = np.kron(wave / math.sqrt(nfreq), np.eye(8)).astype(np.float32)
        hi = flat.astype(jnp.bfloat16)
        lo = (flat - hi.astype(np.float32)).astype(jnp.bfloat16)
        parts.append(np.concatenate([hi, hi, lo], axis=1))
    return np.stack(parts)


def tree(z0, y0, depth):
    last = depth - 1
    if z0 == 0:
        steps = [(0, 2), (2, 3), (2, 1)]
    elif z0 == last:
        steps = [(last, last - 2), (last - 2, last - 3), (last - 2, last - 1)]
    elif z0 == 1:
        steps = [(1, 2), (2, 3), (1, 0)]
    else:
        steps = [(2, 1), (1, 0), (2, 3)]
    back = z0 + 1 if z0 < last else z0 - 1
    halves = []
    for half in (0, 1):
        line = (y0 + half) % 2
        copies = [((z0, y0), (z0, line))] if half else []
        copies += [((z, line), (w, line)) for z, w in steps]
        copies += [((z, line), (z, 1 - line)) for z in range(depth) if z != z0]
        if half == 0:
            copies.append(((back, 1 - y0), (z0, 1 - y0)))
        halves.append(copies)
    return halves


def plan(chip, depth):
    owner = divmod(chip, 2)
    devices = 4 * depth
    targets = [[] for _ in range(devices)]
    parent = [-1] * devices
    hops = [0] * devices
    for half, copies in enumerate(tree(*owner, depth)):
        number = lambda at: 4 * at[0] + 2 * at[1] + half
        for source, target in copies:
            targets[number(source)].append(number(target))
            parent[number(target)] = number(source)
        for device in range(half, devices, 2):
            at = device
            while parent[at] >= 0:
                hops[device] += 1
                at = parent[at]
    return targets, parent, hops


def broadcast_kernel(
    plans, owner_ref, start_ref, survey_ref, out_ref,
    pan, swap, block, load_sem, recv_sem, send_sem, swap_sem, core_send, core_recv, out_sem,
):
    me = lax.axis_index("shot")
    c = me % 2
    peer = me + 1 - 2 * c
    tiles, bins = block.shape[0], block.shape[2]
    count = tiles * bins
    tile = block.shape[4]

    def pick(values):
        total = jnp.int32(0)
        for device, value in enumerate(values):
            if value:
                total = total + jnp.where(me == device, jnp.int32(value), jnp.int32(0))
        return total

    root, use, target, parent, lag = [], [], [], [], []
    for p, (targets, parents, hops) in enumerate(plans):
        root.append(pick([int(at < 0) for at in parents]) == 1)
        parent.append(pick([max(at, 0) for at in parents]))
        use.append([pick([int(len(t) > s) for t in targets]) == 1 for s in range(SLOTS)])
        target.append([pick([t[s] if len(t) > s else 0 for t in targets]) for s in range(SLOTS)])
        others = plans[1 - p][2]
        lag.append(pick([LAG * max(0, mine - other) for mine, other in zip(hops, others)]))
    sends = pick([len(first) + len(second) for first, second in zip(plans[0][0], plans[1][0])])
    some = root[0] | root[1]

    def load(j):
        return pltpu.make_async_copy(
            survey_ref.at[:, :, :, pl.ds(j * tile, tile)], block.at[j], load_sem.at[j]
        )

    @pl.when(some)
    def _():
        for j in range(tiles):
            load(j).start()

    def remote(source, at, send, arrive, device):
        return pltpu.make_async_remote_copy(
            src_ref=source,
            dst_ref=pan.at[at],
            send_sem=send,
            recv_sem=arrive,
            device_id={"shot": device},
            device_id_type=pl.DeviceIdType.MESH,
        )

    def exchange(p, k):
        return remote(swap.at[p, k], (p, 1 - c, k), swap_sem.at[p], recv_sem.at[p, k], peer)

    def forward(p, s, k):
        at = (p, c, k)
        return remote(pan.at[at], at, send_sem.at[p, s, k % WINDOW], recv_sem.at[p, k], target[p][s])

    def share(p, at):
        return remote(pan.at[at], at, core_send.at[p], core_recv.at[p], peer)

    def rows(p, half, k):
        j, f = k // bins, k % bins
        low, high = block[j, half, f, :PANEL, :], block[j, half, f, PANEL:, :]
        return jnp.where(start_ref[p] == 0, low, high)

    def offer(p, k):
        swap[p, k] = rows(p, 1 - c, k)
        exchange(p, k).start()

    barrier = pltpu.get_barrier_semaphore()
    for p in range(STEPS):
        @pl.when(jnp.logical_not(root[p]))
        def _():
            pl.semaphore_signal(
                barrier, inc=1, device_id={"shot": parent[p]}, device_id_type=pl.DeviceIdType.MESH
            )
    pl.semaphore_signal(barrier, inc=1, device_id={"shot": peer}, device_id_type=pl.DeviceIdType.MESH)
    pl.semaphore_wait(barrier, sends + 1)

    @pl.when(some)
    def _():
        for j in range(tiles):
            load(j).wait()

    for p in range(STEPS):
        @pl.when(root[p])
        def _():
            for k in range(AHEAD):
                offer(p, k)

    def step(t, carry):
        for p in range(STEPS):
            k = t - lag[p]

            @pl.when((k >= 0) & (k < count))
            def _():
                @pl.when(root[p] & (k < count - AHEAD))
                def _():
                    offer(p, k + AHEAD)

                at = (p, c, k)
                remote(pan.at[at], at, core_send.at[p], recv_sem.at[p, k], peer).wait_recv()

                @pl.when(root[p])
                def _():
                    pan[p, c, k] = jnp.where(owner_ref[p] == c, rows(p, c, k), pan[p, c, k])

                for s in range(SLOTS):
                    @pl.when(use[p][s])
                    def _():
                        @pl.when(k >= WINDOW)
                        def _():
                            forward(p, s, k - WINDOW).wait_send()

                        forward(p, s, k).start()

                share(p, at).start()
        return carry

    most = max(
        abs(first - second) for first, second in zip(plans[0][2], plans[1][2])
    )
    lax.fori_loop(0, count + LAG * most, step, 0)

    for p in range(STEPS):
        pltpu.make_async_copy(pan.at[p, c], out_ref.at[p, c], out_sem.at[p, 0]).start()
    for p in range(STEPS):
        share(p, (p, 1 - c)).wait_recv()
        pltpu.make_async_copy(pan.at[p, 1 - c], out_ref.at[p, 1 - c], out_sem.at[p, 1]).start()
    for p in range(STEPS):
        for s in range(SLOTS):
            @pl.when(use[p][s])
            def _():
                for k in range(count - WINDOW, count):
                    forward(p, s, k).wait_send()

        share(p, (p, c)).wait_send()

        @pl.when(root[p])
        def _():
            remote(swap.at[p], (p, 1 - c), swap_sem.at[p], core_recv.at[p], peer).wait_send()

        pltpu.make_async_copy(pan.at[p, c], out_ref.at[p, c], out_sem.at[p, 0]).wait()
        pltpu.make_async_copy(pan.at[p, 1 - c], out_ref.at[p, 1 - c], out_sem.at[p, 1]).wait()


def broadcast_rows(survey, chips, cores, offsets, shots):
    _, bins, height, width = survey.shape
    tile = min(256, width)
    tiles = width // tile
    depth = shots // 4
    whole = (STEPS, 2, tiles * bins, PANEL, tile)
    pairs = [(i, j) for i in range(shots // 2) for j in range(i, shots // 2)]
    numbers = np.zeros((shots // 2, shots // 2), np.int32)
    for number, (i, j) in enumerate(pairs):
        numbers[i, j] = number

    def call(number, pair):
        plans = [plan(chip, depth) for chip in pair]
        return pl.pallas_call(
            functools.partial(broadcast_kernel, plans),
            out_shape=jax.ShapeDtypeStruct(whole, survey.dtype),
            in_specs=[
                pl.BlockSpec(memory_space=pltpu.SMEM),
                pl.BlockSpec(memory_space=pltpu.SMEM),
                pl.BlockSpec(memory_space=pl.ANY),
            ],
            out_specs=pl.BlockSpec(memory_space=pl.ANY),
            scratch_shapes=[
                pltpu.VMEM(whole, survey.dtype),
                pltpu.VMEM((STEPS,) + whole[2:], survey.dtype),
                pltpu.VMEM((tiles, 2, bins, height, tile), survey.dtype),
                pltpu.SemaphoreType.DMA((tiles,)),
                pltpu.SemaphoreType.DMA((STEPS, tiles * bins)),
                pltpu.SemaphoreType.DMA((STEPS, SLOTS, WINDOW)),
                pltpu.SemaphoreType.DMA((STEPS,)),
                pltpu.SemaphoreType.DMA((STEPS,)),
                pltpu.SemaphoreType.DMA((STEPS,)),
                pltpu.SemaphoreType.DMA((STEPS, 2)),
            ],
            compiler_params=pltpu.CompilerParams(
                collective_id=number, has_side_effects=True, vmem_limit_bytes=40 << 20
            ),
            name="rows_from_%d_%d" % pair,
        )

    calls = [call(number, pair) for number, pair in enumerate(pairs)]
    return lax.switch(jnp.asarray(numbers)[chips[0], chips[1]], calls, cores, offsets, survey)


def split(array):
    hi = array.astype(jnp.bfloat16)
    return hi, (array - hi.astype(jnp.float32)).astype(jnp.bfloat16)


def dot(left, right):
    return jnp.dot(left, right, preferred_element_type=jnp.float32)


def predict_kernel(
    own_ref, mine_ref, other_ref, row_ref, table_ref, out_ref,
    left_hi, left_lo, freq_ref,
):
    nfreq = mine_ref.shape[1]
    rows = mine_ref.shape[2]
    tile = out_ref.shape[2]

    @pl.when(pl.program_id(0) == 0)
    def _():
        lane = lax.broadcasted_iota(jnp.int32, (rows, 2 * PANEL), 1)
        own = jnp.where(lane < PANEL, own_ref[0], own_ref[1]) == 1
        for f in range(nfreq):
            real = jnp.where(own, mine_ref[0, f], other_ref[0, f])
            imag = jnp.where(own, mine_ref[1, f], other_ref[1, f])
            cos, sin = middle(f)
            real, imag = real * cos - imag * sin, real * sin + imag * cos
            top = jnp.concatenate([real, -imag], axis=1)
            low = jnp.concatenate([imag, real], axis=1)
            hi, lo = split(jnp.concatenate([top, low], axis=0))
            left_hi[f] = hi
            left_lo[f] = lo

    for f in range(nfreq):
        right = jnp.concatenate(
            [row_ref[0, 0, f], row_ref[1, 0, f], row_ref[0, 1, f], row_ref[1, 1, f]], axis=0
        )
        hi, lo = split(right)
        both = dot(left_hi[f], hi) + dot(left_lo[f], hi) + dot(left_hi[f], lo)
        freq_ref[f] = both[:rows]
        freq_ref[nfreq + f] = both[rows:]

    half = SAMPLES // 2
    for g in range(rows // 8):
        at = slice(8 * g, 8 * g + 8)
        waves = []
        for i in (0, 1):
            part = freq_ref[i * nfreq : (i + 1) * nfreq, at, :].reshape(8 * nfreq, tile)
            hi, lo = split(part)
            waves.append(dot(table_ref[i], jnp.concatenate([hi, lo, hi], axis=0)))
        even, odd = waves
        out_ref[half:, at, :] = (even - odd).reshape(half, 8, tile)
        early = even + odd
        for j in range(half):
            out_ref[half - 1 - j, at, :] = early[8 * j : 8 * j + 8]


def predict(own, mine, other, rows):
    _, nfreq, height, _ = mine.shape
    tile = rows.shape[4]
    cols = tile * rows.shape[2] // nfreq
    big = jnp.asarray(kron_tables(nfreq))
    whole = pl.BlockSpec(mine.shape, lambda j: (0, 0, 0, 0))
    row_spec = pl.BlockSpec((STEPS, 2, nfreq, PANEL, tile), lambda j: (0, 0, j, 0, 0))
    return pl.pallas_call(
        predict_kernel,
        grid=(cols // tile,),
        out_shape=jax.ShapeDtypeStruct((SAMPLES, height, cols), jnp.float32),
        in_specs=[
            pl.BlockSpec(memory_space=pltpu.SMEM),
            whole,
            whole,
            row_spec,
            pl.BlockSpec(big.shape, lambda j: (0, 0, 0)),
        ],
        out_specs=pl.BlockSpec((SAMPLES, height, tile), lambda j: (0, 0, j)),
        scratch_shapes=[
            pltpu.VMEM((nfreq, 2 * height, 4 * PANEL), jnp.bfloat16),
            pltpu.VMEM((nfreq, 2 * height, 4 * PANEL), jnp.bfloat16),
            pltpu.VMEM((2 * nfreq, height, tile), jnp.float32),
        ],
        compiler_params=pltpu.CompilerParams(vmem_limit_bytes=48 << 20),
        name="predict",
    )(own, mine, other, rows, big)


def fetch_rows(source, start, shot_rows):
    length = min(shot_rows, PANEL)
    pieces = []
    for index_piece in range(PANEL // length):
        first = start + index_piece * length
        owner = first // shot_rows
        offset = first % shot_rows
        piece = lax.dynamic_slice_in_dim(source, offset, length, 2)
        pieces.append(from_root(piece, "shot", owner))
    return jnp.concatenate(pieces, axis=2)


def by_tile(rows):
    _, bins, height, width = rows.shape
    tile = min(256, width)
    cut = rows.reshape(2, bins, height, width // tile, tile)
    return cut.transpose(0, 3, 1, 2, 4).reshape(2, -1, height, tile)


def shards(direct, shots, recs, survey, panel_index):
    shot_rows = survey.shape[2]
    rec_cols = survey.shape[3]
    if direct:
        panel_index = jnp.stack([jnp.min(panel_index), jnp.max(panel_index)])
    starts = [panel_index[step] * PANEL for step in range(STEPS)]
    columns = [
        lax.dynamic_slice_in_dim(survey, start % rec_cols, PANEL, 3) for start in starts
    ]
    owners = jnp.stack([start // rec_cols for start in starts])
    me = lax.axis_index("rec")
    mine = jnp.concatenate(columns, axis=3)
    if direct:
        other = lax.ppermute(mine, "rec", [(0, 1), (1, 0)])
        own = (owners == me).astype(jnp.int32)
        places = panel_index * PANEL // shot_rows
        offsets = panel_index * PANEL % shot_rows
        rows = broadcast_rows(survey, places // 2, places % 2, offsets, shots)
    else:
        wanted = jnp.repeat(owners == me, PANEL, total_repeat_length=STEPS * PANEL)
        mine = lax.psum(jnp.where(wanted, mine, 0.0), "rec")
        other = mine
        own = jnp.ones((STEPS,), jnp.int32)
        rows = jnp.stack([by_tile(fetch_rows(survey, start, shot_rows)) for start in starts])
    return predict(own, mine, other, rows)


def solution(mesh):
    shots, recs = mesh.shape["shot"], mesh.shape["rec"]
    direct = (shots, recs) == (16, 2)
    return jax.shard_map(
        functools.partial(shards, direct, shots, recs),
        mesh=mesh,
        in_specs=(P(None, None, "shot", "rec"), P()),
        out_specs=P(None, "shot", "rec"),
        check_vma=False,
    )
```

```python
import functools
import math

import jax
import jax.numpy as jnp
import numpy as np
from jax import lax
from jax.experimental import pallas as pl
from jax.experimental.pallas import tpu as pltpu
from jax.sharding import PartitionSpec as P

FIRST_BIN = 8
TRACE_LEN = 400
SAMPLES = 64
PANEL = 64
STEPS = 2
SLOTS = 3
WINDOW = 4
LAG = 3
BEGIN = 24
RATE = 4
AHEAD = 4


def from_root(array, axis, root):
    mine = lax.axis_index(axis) == root
    return lax.psum(jnp.where(mine, array, jnp.zeros_like(array)), axis)


def middle(f):
    angle = 2.0 * math.pi * (f + FIRST_BIN) * (0.5 * (SAMPLES - 1)) / TRACE_LEN
    return math.cos(angle), math.sin(angle)


def kron_tables(nfreq):
    moments = np.arange(SAMPLES // 2) + 0.5
    bins = np.arange(nfreq) + FIRST_BIN
    angle = moments[:, None] * bins[None, :] * (2.0 * math.pi / TRACE_LEN)
    parts = []
    for wave in (np.cos(angle), np.sin(angle)):
        flat = np.kron(wave / math.sqrt(nfreq), np.eye(8)).astype(np.float32)
        hi = flat.astype(jnp.bfloat16)
        lo = (flat - hi.astype(np.float32)).astype(jnp.bfloat16)
        parts.append(np.concatenate([hi, hi, lo], axis=1))
    return np.stack(parts)


def tree(z0, y0, depth):
    last = depth - 1
    if z0 == 0:
        steps = [(0, 2), (2, 3), (2, 1)]
    elif z0 == last:
        steps = [(last, last - 2), (last - 2, last - 3), (last - 2, last - 1)]
    elif z0 == 1:
        steps = [(1, 2), (2, 3), (1, 0)]
    else:
        steps = [(2, 1), (1, 0), (2, 3)]
    back = z0 + 1 if z0 < last else z0 - 1
    halves = []
    for half in (0, 1):
        line = (y0 + half) % 2
        copies = [((z0, y0), (z0, line))] if half else []
        copies += [((z, line), (w, line)) for z, w in steps]
        copies += [((z, line), (z, 1 - line)) for z in range(depth) if z != z0]
        if half == 0:
            copies.append(((back, 1 - y0), (z0, 1 - y0)))
        halves.append(copies)
    return halves


def plan(chip, depth):
    owner = divmod(chip, 2)
    devices = 4 * depth
    targets = [[] for _ in range(devices)]
    parent = [-1] * devices
    hops = [0] * devices
    for half, copies in enumerate(tree(*owner, depth)):
        number = lambda at: 4 * at[0] + 2 * at[1] + half
        for source, target in copies:
            targets[number(source)].append(number(target))
            parent[number(target)] = number(source)
        for device in range(half, devices, 2):
            at = device
            while parent[at] >= 0:
                hops[device] += 1
                at = parent[at]
    return targets, parent, hops


def split(array):
    hi = array.astype(jnp.bfloat16)
    return hi, (array - hi.astype(jnp.float32)).astype(jnp.bfloat16)


def dot(left, right):
    return jnp.dot(left, right, preferred_element_type=jnp.float32)


def product_kernel(
    plans, panel_ref, survey_ref, out_ref,
    pan, swap, block, mine, other, left_hi, left_lo, freq,
    load_sem, recv_sem, send_sem, swap_sem, core_send, core_recv, side_sem, out_sem,
):
    me, rec = lax.axis_index("shot"), lax.axis_index("rec")
    c = me % 2
    peer = me + 1 - 2 * c
    tiles, _, bins, height, tile = block.shape
    count = tiles * bins
    low, high = panel_ref[0], panel_ref[1]
    panels = (jnp.minimum(low, high), jnp.maximum(low, high))

    def pick(values):
        total = jnp.int32(0)
        for device, value in enumerate(values):
            if value:
                total = total + jnp.where(me == device, jnp.int32(value), jnp.int32(0))
        return total

    root, use, target, parent, lag = [], [], [], [], []
    for p, (targets, parents, hops) in enumerate(plans):
        root.append(pick([int(at < 0) for at in parents]) == 1)
        parent.append(pick([max(at, 0) for at in parents]))
        use.append([pick([int(len(t) > s) for t in targets]) == 1 for s in range(SLOTS)])
        target.append([pick([t[s] if len(t) > s else 0 for t in targets]) for s in range(SLOTS)])
        others = plans[1 - p][2]
        lag.append(pick([LAG * max(0, mine - other) for mine, other in zip(hops, others)]))
    sends = pick([len(first) + len(second) for first, second in zip(plans[0][0], plans[1][0])])
    behind = [
        LAG * (max(h[2 * (at // 2) + i] for _, _, h in plans for i in (0, 1)) - min(h[at] for _, _, h in plans)) + 2
        for at in range(len(plans[0][0]))
    ]
    delay = pick(behind)

    def load(j):
        return pltpu.make_async_copy(
            survey_ref.at[:, :, :, pl.ds(j * tile, tile)], block.at[j], load_sem.at[j]
        )

    for j in range(tiles):
        load(j).start()

    def remote(source, target, send, arrive, device):
        return pltpu.make_async_remote_copy(
            src_ref=source,
            dst_ref=target,
            send_sem=send,
            recv_sem=arrive,
            device_id=device,
            device_id_type=pl.DeviceIdType.MESH,
        )

    def exchange(p, k):
        to = pan.at[p, 1 - c, k]
        return remote(swap.at[p, k], to, swap_sem.at[p], recv_sem.at[p, k], {"shot": peer})

    def forward(p, s, k):
        piece = pan.at[p, c, k]
        send = send_sem.at[p, s, k % WINDOW]
        return remote(piece, piece, send, recv_sem.at[p, k], {"shot": target[p][s]})

    def share(p, half, k):
        piece = pan.at[p, half, k]
        return remote(piece, piece, core_send.at[p], core_recv.at[p, k], {"shot": peer})

    places = [panels[p] // 2 % (tiles * tile // (2 * PANEL)) for p in range(STEPS)]
    odd = [panels[p] % 2 for p in range(STEPS)]

    def rows(p, half, k):
        j, f = k // bins, k % bins
        first, second = block[j, half, f, :PANEL, :], block[j, half, f, PANEL:, :]
        return jnp.where(panels[p] % 2 == 0, first, second)

    def offer(p, k):
        swap[p, k] = rows(p, 1 - c, k)
        exchange(p, k).start()

    def side(at):
        return remote(mine.at[at], other.at[at], side_sem.at[0], side_sem.at[1], {"rec": 1 - rec})

    def columns(at):
        lane = lax.broadcasted_iota(jnp.int32, (height, 2 * PANEL), 1)
        i, f = at // bins, at % bins
        parts = [jnp.zeros((height, 2 * PANEL), jnp.float32)] * STEPS
        for j in range(tiles):
            for first in range(0, tile, 2 * PANEL):
                place = (j * tile + first) // (2 * PANEL)
                whole = block[j, i, f, :, first : first + 2 * PANEL]
                parts = [jnp.where(places[p] == place, whole, parts[p]) for p in range(STEPS)]
        for p in range(STEPS):
            parts[p] = jnp.where(odd[p] == p, parts[p], pltpu.roll(parts[p], PANEL, 1))
        mine[at] = jnp.where(lane < PANEL, parts[0], parts[1])
        side(at).start()

    def left(f):
        lane = lax.broadcasted_iota(jnp.int32, (height, 2 * PANEL), 1)
        panel = jnp.where(lane < PANEL, panels[0], panels[1])
        own = panel * PANEL // (tiles * tile) == rec
        real = jnp.where(own, mine[f], other[f])
        imag = jnp.where(own, mine[bins + f], other[bins + f])
        cos, sin = jnp.float32(0), jnp.float32(0)
        for g in range(bins):
            cos = jnp.where(f == g, jnp.float32(middle(g)[0]), cos)
            sin = jnp.where(f == g, jnp.float32(middle(g)[1]), sin)
        real, imag = real * cos - imag * sin, real * sin + imag * cos
        top = jnp.concatenate([real, -imag], axis=1)
        bottom = jnp.concatenate([imag, real], axis=1)
        hi, lo = split(jnp.concatenate([top, bottom], axis=0))
        left_hi[f] = hi
        left_lo[f] = lo

    def multiply(k):
        j, f = k // bins, k % bins
        right = jnp.concatenate([pan[0, 0, k], pan[1, 0, k], pan[0, 1, k], pan[1, 1, k]], axis=0)
        hi, lo = split(right)
        both = dot(left_hi[f], hi) + dot(left_lo[f], hi) + dot(left_hi[f], lo)
        freq[j, f, 0] = both[:height]
        freq[j, f, 1] = both[height:]
        pltpu.make_async_copy(freq.at[j, f], out_ref.at[j, f], out_sem).start()

    barrier = pltpu.get_barrier_semaphore()
    for p in range(STEPS):
        @pl.when(jnp.logical_not(root[p]))
        def _():
            pl.semaphore_signal(
                barrier, inc=1, device_id={"shot": parent[p]}, device_id_type=pl.DeviceIdType.MESH
            )
    for device in ({"shot": peer}, {"rec": 1 - rec}):
        pl.semaphore_signal(barrier, inc=1, device_id=device, device_id_type=pl.DeviceIdType.MESH)
    pl.semaphore_wait(barrier, sends + 2)

    for j in range(tiles):
        load(j).wait()

    for p in range(STEPS):
        @pl.when(root[p])
        def _():
            for k in range(AHEAD):
                offer(p, k)

    def done(t):
        return jnp.maximum(jnp.minimum(jnp.minimum(RATE * (t - BEGIN), t - delay), count), 0)

    def step(t, carry):
        for p in range(STEPS):
            k = t - lag[p]

            @pl.when((k >= 0) & (k < count))
            def _():
                @pl.when(root[p] & (k < count - AHEAD))
                def _():
                    offer(p, k + AHEAD)

                piece = pan.at[p, c, k]
                remote(piece, piece, core_send.at[p], recv_sem.at[p, k], {"shot": peer}).wait_recv()

                @pl.when(root[p])
                def _():
                    ours = panels[p] // 2 % 2 == c
                    pan[p, c, k] = jnp.where(ours, rows(p, c, k), pan[p, c, k])

                for s in range(SLOTS):
                    @pl.when(use[p][s])
                    def _():
                        @pl.when(k >= WINDOW)
                        def _():
                            forward(p, s, k - WINDOW).wait_send()

                        forward(p, s, k).start()

                share(p, c, k).start()

        @pl.when((t >= 1) & (t <= bins))
        def _():
            columns(2 * t - 2)
            columns(2 * t - 1)

        @pl.when(t == BEGIN - bins // 2)
        def _():
            remote(mine, other, side_sem.at[0], side_sem.at[1], {"rec": 1 - rec}).wait_recv()

        @pl.when((t >= BEGIN - bins // 2) & (t < BEGIN))
        def _():
            left(2 * (t - BEGIN) + bins)
            left(2 * (t - BEGIN) + bins + 1)

        first, past = done(t), done(t + 1)
        def product_of(k, carry):
            for p in range(STEPS):
                share(p, 1 - c, k).wait_recv()
            multiply(k)
            return carry

        lax.fori_loop(done(t), done(t + 1), product_of, 0)
        return carry

    lax.fori_loop(0, max(count + max(behind), BEGIN + count // RATE), step, 0)

    for p in range(STEPS):
        for s in range(SLOTS):
            @pl.when(use[p][s])
            def _():
                for k in range(count - WINDOW, count):
                    forward(p, s, k).wait_send()

        remote(pan.at[p, c], pan.at[p, c], core_send.at[p], recv_sem.at[p, 0], {"shot": peer}).wait_send()

        @pl.when(root[p])
        def _():
            to = pan.at[p, 1 - c]
            remote(swap.at[p], to, swap_sem.at[p], recv_sem.at[p, 0], {"shot": peer}).wait_send()
    remote(mine, other, side_sem.at[0], side_sem.at[1], {"rec": 1 - rec}).wait_send()
    pltpu.make_async_copy(freq, out_ref, out_sem).wait()


def number_kernel(chips, each, panel_ref, out_ref):
    first, second = panel_ref[0], panel_ref[1]
    i = jnp.minimum(first, second) // each
    j = jnp.maximum(first, second) // each
    out_ref[0] = i * chips - i * (i + 1) // 2 + j


def product(survey, panel_index, shots):
    _, bins, height, width = survey.shape
    tile = min(256, width)
    tiles = width // tile
    depth = shots // 4
    chips = shots // 2
    pieces = (STEPS, 2, tiles * bins, PANEL, tile)
    whole = (tiles, bins, 2, height, tile)
    column = (2 * bins, height, STEPS * PANEL)
    factor = pltpu.VMEM((bins, 2 * height, 2 * STEPS * PANEL), jnp.bfloat16)

    def call(number, pair):
        plans = [plan(chip, depth) for chip in pair]
        return pl.pallas_call(
            functools.partial(product_kernel, plans),
            out_shape=jax.ShapeDtypeStruct(whole, survey.dtype),
            in_specs=[pl.BlockSpec(memory_space=pltpu.SMEM), pl.BlockSpec(memory_space=pl.ANY)],
            out_specs=pl.BlockSpec(memory_space=pl.ANY),
            scratch_shapes=[
                pltpu.VMEM(pieces, survey.dtype),
                pltpu.VMEM((STEPS,) + pieces[2:], survey.dtype),
                pltpu.VMEM((tiles, 2, bins, height, tile), survey.dtype),
                pltpu.VMEM(column, survey.dtype),
                pltpu.VMEM(column, survey.dtype),
                factor,
                factor,
                pltpu.VMEM(whole, survey.dtype),
                pltpu.SemaphoreType.DMA((tiles,)),
                pltpu.SemaphoreType.DMA((STEPS, tiles * bins)),
                pltpu.SemaphoreType.DMA((STEPS, SLOTS, WINDOW)),
                pltpu.SemaphoreType.DMA((STEPS,)),
                pltpu.SemaphoreType.DMA((STEPS,)),
                pltpu.SemaphoreType.DMA((STEPS, tiles * bins)),
                pltpu.SemaphoreType.DMA((2,)),
                pltpu.SemaphoreType.DMA,
            ],
            compiler_params=pltpu.CompilerParams(
                collective_id=number, has_side_effects=True, vmem_limit_bytes=48 << 20
            ),
            name="product_%d_%d" % pair,
        )

    pairs = [(i, j) for i in range(chips) for j in range(i, chips)]
    calls = [call(number, pair) for number, pair in enumerate(pairs)]
    number = pl.pallas_call(
        functools.partial(number_kernel, chips, 2 * height // PANEL),
        out_shape=jax.ShapeDtypeStruct((1,), jnp.int32),
        in_specs=[pl.BlockSpec(memory_space=pltpu.SMEM)],
        out_specs=pl.BlockSpec(memory_space=pltpu.SMEM),
        name="number",
    )(panel_index)
    freq = lax.switch(number[0], calls, panel_index, survey)
    return expand(freq)


def expand_kernel(freq_ref, table_ref, out_ref):
    samples, rows, tile = out_ref.shape
    nfreq = freq_ref.shape[1]
    half = samples // 2
    for g in range(rows // 8):
        at = slice(8 * g, 8 * g + 8)
        waves = []
        for i in (0, 1):
            part = freq_ref[0, :, i, at, :].reshape(8 * nfreq, tile)
            hi, lo = split(part)
            waves.append(dot(table_ref[i], jnp.concatenate([hi, lo, hi], axis=0)))
        even, odd = waves
        out_ref[half:, at, :] = (even - odd).reshape(half, 8, tile)
        early = even + odd
        for j in range(half):
            out_ref[half - 1 - j, at, :] = early[8 * j : 8 * j + 8]


def expand(freq):
    tiles, bins, _, height, tile = freq.shape
    big = jnp.asarray(kron_tables(bins))
    return pl.pallas_call(
        expand_kernel,
        grid=(tiles,),
        out_shape=jax.ShapeDtypeStruct((SAMPLES, height, tiles * tile), jnp.float32),
        in_specs=[
            pl.BlockSpec((1,) + freq.shape[1:], lambda j: (j, 0, 0, 0, 0)),
            pl.BlockSpec(big.shape, lambda j: (0, 0, 0)),
        ],
        out_specs=pl.BlockSpec((SAMPLES, height, tile), lambda j: (0, 0, j)),
        compiler_params=pltpu.CompilerParams(vmem_limit_bytes=40 << 20),
        name="expand",
    )(freq, big)


def predict_kernel(
    own_ref, mine_ref, other_ref, row0_ref, row1_ref, table_ref, out_ref,
    left_hi, left_lo, freq_ref,
):
    nfreq = mine_ref.shape[1]
    rows = mine_ref.shape[2]
    tile = out_ref.shape[2]

    @pl.when(pl.program_id(0) == 0)
    def _():
        lane = lax.broadcasted_iota(jnp.int32, (rows, 2 * PANEL), 1)
        own = jnp.where(lane < PANEL, own_ref[0], own_ref[1]) == 1
        for f in range(nfreq):
            real = jnp.where(own, mine_ref[0, f], other_ref[0, f])
            imag = jnp.where(own, mine_ref[1, f], other_ref[1, f])
            cos, sin = middle(f)
            real, imag = real * cos - imag * sin, real * sin + imag * cos
            top = jnp.concatenate([real, -imag], axis=1)
            low = jnp.concatenate([imag, real], axis=1)
            hi, lo = split(jnp.concatenate([top, low], axis=0))
            left_hi[f] = hi
            left_lo[f] = lo

    for f in range(nfreq):
        right = jnp.concatenate(
            [row0_ref[0, f], row1_ref[0, f], row0_ref[1, f], row1_ref[1, f]], axis=0
        )
        hi, lo = split(right)
        both = dot(left_hi[f], hi) + dot(left_lo[f], hi) + dot(left_hi[f], lo)
        freq_ref[f] = both[:rows]
        freq_ref[nfreq + f] = both[rows:]

    half = SAMPLES // 2
    for g in range(rows // 8):
        at = slice(8 * g, 8 * g + 8)
        waves = []
        for i in (0, 1):
            part = freq_ref[i * nfreq : (i + 1) * nfreq, at, :].reshape(8 * nfreq, tile)
            hi, lo = split(part)
            waves.append(dot(table_ref[i], jnp.concatenate([hi, lo, hi], axis=0)))
        even, odd = waves
        out_ref[half:, at, :] = (even - odd).reshape(half, 8, tile)
        early = even + odd
        for j in range(half):
            out_ref[half - 1 - j, at, :] = early[8 * j : 8 * j + 8]


def predict(own, mine, other, row0, row1):
    _, nfreq, rows, width = mine.shape
    cols = row0.shape[3]
    tile = min(256, cols)
    big = jnp.asarray(kron_tables(nfreq))
    whole = pl.BlockSpec(mine.shape, lambda j: (0, 0, 0, 0))
    row_spec = pl.BlockSpec((2, nfreq, PANEL, tile), lambda j: (0, 0, 0, j))
    return pl.pallas_call(
        predict_kernel,
        grid=(cols // tile,),
        out_shape=jax.ShapeDtypeStruct((SAMPLES, rows, cols), jnp.float32),
        in_specs=[
            pl.BlockSpec(memory_space=pltpu.SMEM),
            whole,
            whole,
            row_spec,
            row_spec,
            pl.BlockSpec(big.shape, lambda j: (0, 0, 0)),
        ],
        out_specs=pl.BlockSpec((SAMPLES, rows, tile), lambda j: (0, 0, j)),
        scratch_shapes=[
            pltpu.VMEM((nfreq, 2 * rows, 4 * PANEL), jnp.bfloat16),
            pltpu.VMEM((nfreq, 2 * rows, 4 * PANEL), jnp.bfloat16),
            pltpu.VMEM((2 * nfreq, rows, tile), jnp.float32),
        ],
        compiler_params=pltpu.CompilerParams(vmem_limit_bytes=48 << 20),
        name="predict",
    )(own, mine, other, row0, row1, big)


def fetch_rows(source, start, shot_rows):
    length = min(shot_rows, PANEL)
    pieces = []
    for index_piece in range(PANEL // length):
        first = start + index_piece * length
        owner = first // shot_rows
        offset = first % shot_rows
        piece = lax.dynamic_slice_in_dim(source, offset, length, 2)
        pieces.append(from_root(piece, "shot", owner))
    return jnp.concatenate(pieces, axis=2)


def gathered(survey, panel_index):
    shot_rows = survey.shape[2]
    rec_cols = survey.shape[3]
    starts = [panel_index[step] * PANEL for step in range(STEPS)]
    columns = [
        lax.dynamic_slice_in_dim(survey, start % rec_cols, PANEL, 3) for start in starts
    ]
    owners = jnp.stack([start // rec_cols for start in starts])
    mine = jnp.concatenate(columns, axis=3)
    wanted = jnp.repeat(
        owners == lax.axis_index("rec"), PANEL, total_repeat_length=STEPS * PANEL
    )
    mine = lax.psum(jnp.where(wanted, mine, 0.0), "rec")
    own = jnp.ones((STEPS,), jnp.int32)
    rows = [fetch_rows(survey, start, shot_rows) for start in starts]
    return predict(own, mine, mine, rows[0], rows[1])


def solution(mesh):
    shots, recs = mesh.shape["shot"], mesh.shape["rec"]

    def shards(survey, panel_index):
        if (shots, recs) == (16, 2):
            return product(survey, panel_index, shots)
        return gathered(survey, panel_index)

    return jax.shard_map(
        shards,
        mesh=mesh,
        in_specs=(P(None, None, "shot", "rec"), P()),
        out_specs=P(None, "shot", "rec"),
        check_vma=False,
    )
```

```python
import functools
import math

import jax
import jax.numpy as jnp
import numpy as np
from jax import lax
from jax.experimental import pallas as pl
from jax.experimental.pallas import tpu as pltpu
from jax.sharding import PartitionSpec as P

FIRST_BIN = 8
TRACE_LEN = 400
SAMPLES = 64
PANEL = 64
STEPS = 2
SLOTS = 3
WINDOW = 4
LAG = 3
BEGIN = 24
RATE = 4
AHEAD = 4
FIELDS = (0, 2, 6, 7, 12, 17, 21, 25, 29)


def from_root(array, axis, root):
    mine = lax.axis_index(axis) == root
    return lax.psum(jnp.where(mine, array, jnp.zeros_like(array)), axis)


def middle(f):
    angle = 2.0 * math.pi * (f + FIRST_BIN) * (0.5 * (SAMPLES - 1)) / TRACE_LEN
    return math.cos(angle), math.sin(angle)


def kron_tables(nfreq):
    moments = np.arange(SAMPLES // 2) + 0.5
    bins = np.arange(nfreq) + FIRST_BIN
    angle = moments[:, None] * bins[None, :] * (2.0 * math.pi / TRACE_LEN)
    parts = []
    for wave in (np.cos(angle), np.sin(angle)):
        flat = np.kron(wave / math.sqrt(nfreq), np.eye(8)).astype(np.float32)
        hi = flat.astype(jnp.bfloat16)
        lo = (flat - hi.astype(np.float32)).astype(jnp.bfloat16)
        parts.append(np.concatenate([hi, hi, lo], axis=1))
    return np.stack(parts)


def tree(z0, y0, depth):
    last = depth - 1
    if z0 == 0:
        steps = [(0, 2), (2, 3), (2, 1)]
    elif z0 == last:
        steps = [(last, last - 2), (last - 2, last - 3), (last - 2, last - 1)]
    elif z0 == 1:
        steps = [(1, 2), (2, 3), (1, 0)]
    else:
        steps = [(2, 1), (1, 0), (2, 3)]
    back = z0 + 1 if z0 < last else z0 - 1
    halves = []
    for half in (0, 1):
        line = (y0 + half) % 2
        copies = [((z0, y0), (z0, line))] if half else []
        copies += [((z, line), (w, line)) for z, w in steps]
        copies += [((z, line), (z, 1 - line)) for z in range(depth) if z != z0]
        if half == 0:
            copies.append(((back, 1 - y0), (z0, 1 - y0)))
        halves.append(copies)
    return halves


def plan(chip, depth):
    owner = divmod(chip, 2)
    devices = 4 * depth
    targets = [[] for _ in range(devices)]
    parent = [-1] * devices
    hops = [0] * devices
    for half, copies in enumerate(tree(*owner, depth)):
        number = lambda at: 4 * at[0] + 2 * at[1] + half
        for source, target in copies:
            targets[number(source)].append(number(target))
            parent[number(target)] = number(source)
        for device in range(half, devices, 2):
            at = device
            while parent[at] >= 0:
                hops[device] += 1
                at = parent[at]
    return targets, parent, hops


def split(array):
    hi = array.astype(jnp.bfloat16)
    return hi, (array - hi.astype(jnp.float32)).astype(jnp.bfloat16)


def dot(left, right):
    return jnp.dot(left, right, preferred_element_type=jnp.float32)


def product_kernel(
    plans, panel_ref, survey_ref, out_ref,
    pan, swap, block, mine, other, left_all, freq,
    load_sem, recv_sem, send_sem, swap_sem, core_send, core_recv, side_sem, out_sem,
):
    me, rec = lax.axis_index("shot"), lax.axis_index("rec")
    c = me % 2
    peer = me + 1 - 2 * c
    tiles, _, bins, height, tile = block.shape
    count = tiles * bins
    low, high = panel_ref[0], panel_ref[1]
    panels = (jnp.minimum(low, high), jnp.maximum(low, high))

    depths = [hops for _, _, hops in plans]
    words, delays = [[], []], []
    for at in range(len(depths[0])):
        near = min(hops[at] for hops in depths)
        pair = (2 * (at // 2), 2 * (at // 2) + 1)
        delays.append(LAG * (max(hops[i] for hops in depths for i in pair) - near) + 2)
        for p, (targets, parents, hops) in enumerate(plans):
            fields = [len(targets[at]), max(parents[at], 0), int(parents[at] < 0), LAG * (hops[at] - near), delays[at]]
            fields += targets[at] + [0] * (SLOTS - len(targets[at]))
            words[p].append(sum(value << place for value, place in zip(fields, FIELDS)))

    def both_of(first, second):
        return lambda p: jnp.where(p == 0, first, second)

    word = []
    for p in range(STEPS):
        total = jnp.int32(0)
        for device, value in enumerate(words[p]):
            total = total + jnp.where(me == device, jnp.int32(value), jnp.int32(0))
        word.append(total)

    def field(at):
        width = FIELDS[at + 1] - FIELDS[at]
        parts = [lax.rem(lax.div(w, jnp.int32(1 << FIELDS[at])), jnp.int32(1 << width)) for w in word]
        return both_of(*parts)

    sends, parent, root, lag, delay = [field(at) for at in range(5)]
    targets = [field(5 + s) for s in range(SLOTS)]
    delay = delay(0)
    panel = both_of(*panels)

    def target(p, s):
        found = targets[0](p)
        for other_slot in range(1, SLOTS):
            found = jnp.where(s == other_slot, targets[other_slot](p), found)
        return found

    def each(count, body):
        def turn(at, carry):
            body(at)
            return carry

        lax.fori_loop(0, count, turn, 0)

    def load(j):
        return pltpu.make_async_copy(
            survey_ref.at[:, :, :, pl.ds(pl.multiple_of(j * tile, tile), tile)], block.at[j], load_sem.at[j]
        )

    each(tiles, lambda j: load(j).start())

    def remote(source, target, send, arrive, device):
        return pltpu.make_async_remote_copy(
            src_ref=source,
            dst_ref=target,
            send_sem=send,
            recv_sem=arrive,
            device_id=device,
            device_id_type=pl.DeviceIdType.MESH,
        )

    def exchange(p, k):
        to = pan.at[p, 1 - c, k]
        return remote(swap.at[p, k], to, swap_sem.at[p], recv_sem.at[p, k], {"shot": peer})

    def forward(p, s, k):
        piece = pan.at[p, c, k]
        send = send_sem.at[p, s, k % WINDOW]
        return remote(piece, piece, send, recv_sem.at[p, k], {"shot": target(p, s)})

    def share(p, half, k):
        piece = pan.at[p, half, k]
        return remote(piece, piece, core_send.at[p], core_recv.at[p, k], {"shot": peer})

    places = [panels[p] // 2 % (tiles * tile // (2 * PANEL)) for p in range(STEPS)]
    odd = [panels[p] % 2 for p in range(STEPS)]

    def rows(p, half, k):
        j, f = k // bins, k % bins
        first, second = block[j, half, f, :PANEL, :], block[j, half, f, PANEL:, :]
        return jnp.where(panel(p) % 2 == 0, first, second)

    def offer(p, k):
        swap[p, k] = rows(p, 1 - c, k)
        exchange(p, k).start()

    def side(at):
        return remote(mine.at[at], other.at[at], side_sem.at[0], side_sem.at[1], {"rec": 1 - rec})

    def columns(at):
        lane = lax.broadcasted_iota(jnp.int32, (height, 2 * PANEL), 1)
        i, f = at // bins, at % bins

        def look(j, parts):
            for first in range(0, tile, 2 * PANEL):
                place = j * (tile // (2 * PANEL)) + first // (2 * PANEL)
                whole = block[j, i, f, :, first : first + 2 * PANEL]
                parts = [jnp.where(places[p] == place, whole, parts[p]) for p in range(STEPS)]
            return parts

        nothing = jnp.zeros((height, 2 * PANEL), jnp.float32)
        parts = lax.fori_loop(0, tiles, look, [nothing] * STEPS)
        for p in range(STEPS):
            parts[p] = jnp.where(odd[p] == p, parts[p], pltpu.roll(parts[p], PANEL, 1))
        mine[at] = jnp.where(lane < PANEL, parts[0], parts[1])
        side(at).start()

    def left(f):
        part = height // 2
        lane = lax.broadcasted_iota(jnp.int32, (part, 2 * PANEL), 1)
        place = jnp.where(lane < PANEL, panels[0], panels[1])
        own = place * PANEL // (tiles * tile) == rec
        cos, sin = jnp.float32(0), jnp.float32(0)
        for g in range(bins):
            cos = jnp.where(f == g, jnp.float32(middle(g)[0]), cos)
            sin = jnp.where(f == g, jnp.float32(middle(g)[1]), sin)

        def body(at):
            at = pl.multiple_of(at * part, part)
            line = pl.ds(at, part)
            real = jnp.where(own, mine[f, line], other[f, line])
            imag = jnp.where(own, mine[bins + f, line], other[bins + f, line])
            first, second = real * cos - imag * sin, real * sin + imag * cos
            for start, pair in ((0, [first, -second]), (height, [second, first])):
                hi, lo = split(jnp.concatenate(pair, axis=1))
                left_all[f, pl.ds(start + at, part)] = jnp.concatenate([hi, lo, hi], axis=1)

        each(2, body)

    def multiply(k):
        j, f = k // bins, k % bins
        whole = jnp.concatenate([pan[0, 0, k], pan[1, 0, k], pan[0, 1, k], pan[1, 1, k]], axis=0)
        hi, lo = split(whole)
        both = dot(left_all[f], jnp.concatenate([hi, hi, lo], axis=0))
        freq[j, f, 0] = both[:height]
        freq[j, f, 1] = both[height:]
        pltpu.make_async_copy(freq.at[j, f], out_ref.at[j, f], out_sem).start()

    barrier = pltpu.get_barrier_semaphore()

    def enter(device):
        pl.semaphore_signal(barrier, inc=1, device_id=device, device_id_type=pl.DeviceIdType.MESH)

    def greet(p):
        @pl.when(root(p) == 0)
        def _():
            enter({"shot": parent(p)})

    each(STEPS, greet)
    enter({"shot": peer})
    enter({"rec": 1 - rec})
    pl.semaphore_wait(barrier, sends(0) + sends(1) + 2)

    load(0).wait()

    def done(t):
        return jnp.maximum(jnp.minimum(jnp.minimum(RATE * (t - BEGIN), t - delay), count), 0)

    def pass_on(p, k):
        piece = pan.at[p, c, k]
        remote(piece, piece, core_send.at[p], recv_sem.at[p, k], {"shot": peer}).wait_recv()

        @pl.when(root(p) == 1)
        def _():
            ours = panel(p) // 2 % 2 == c
            pan[p, c, k] = jnp.where(ours, rows(p, c, k), pan[p, c, k])

        def send(s):
            @pl.when(k >= WINDOW)
            def _():
                forward(p, s, k - WINDOW).wait_send()

            forward(p, s, k).start()

        each(sends(p), send)
        share(p, c, k).start()

    def step(t):
        def turn(p):
            k = t - lag(p)

            @pl.when((root(p) == 1) & (k < count - AHEAD))
            def _():
                offer(p, k + AHEAD)

            @pl.when((k >= 0) & (k < count))
            def _():
                pass_on(p, k)

        each(STEPS, turn)

        @pl.when(t == 0)
        def _():
            each(tiles - 1, lambda j: load(j + 1).wait())

        @pl.when((t >= 1) & (t <= bins))
        def _():
            each(2, lambda at: columns(2 * t - 2 + at))

        @pl.when(t == BEGIN - bins // 2)
        def _():
            remote(mine, other, side_sem.at[0], side_sem.at[1], {"rec": 1 - rec}).wait_recv()

        @pl.when((t >= BEGIN - bins // 2) & (t < BEGIN))
        def _():
            each(2, lambda at: left(2 * (t - BEGIN) + bins + at))

        def product_of(k, carry):
            for p in range(STEPS):
                share(p, 1 - c, k).wait_recv()
            multiply(k)
            return carry

        lax.fori_loop(done(t), done(t + 1), product_of, 0)

    each(AHEAD + max(count + max(delays), BEGIN + count // RATE), lambda at: step(at - AHEAD))

    def finish(p):
        def drain(s):
            each(WINDOW, lambda at: forward(p, s, count - WINDOW + at).wait_send())

        each(sends(p), drain)
        remote(pan.at[p, c], pan.at[p, c], core_send.at[p], recv_sem.at[p, 0], {"shot": peer}).wait_send()

        @pl.when(root(p) == 1)
        def _():
            to = pan.at[p, 1 - c]
            remote(swap.at[p], to, swap_sem.at[p], recv_sem.at[p, 0], {"shot": peer}).wait_send()

    each(STEPS, finish)
    remote(mine, other, side_sem.at[0], side_sem.at[1], {"rec": 1 - rec}).wait_send()
    pltpu.make_async_copy(freq, out_ref, out_sem).wait()


def number_kernel(chips, each, panel_ref, out_ref):
    first, second = panel_ref[0], panel_ref[1]
    i = jnp.minimum(first, second) // each
    j = jnp.maximum(first, second) // each
    out_ref[0] = i * chips - i * (i + 1) // 2 + j


def product(survey, panel_index, shots):
    _, bins, height, width = survey.shape
    tile = min(256, width)
    tiles = width // tile
    depth = shots // 4
    chips = shots // 2
    pieces = (STEPS, 2, tiles * bins, PANEL, tile)
    whole = (tiles, bins, 2, height, tile)
    column = (2 * bins, height, STEPS * PANEL)

    def call(number, pair):
        plans = [plan(chip, depth) for chip in pair]
        return pl.pallas_call(
            functools.partial(product_kernel, plans),
            out_shape=jax.ShapeDtypeStruct(whole, survey.dtype),
            in_specs=[pl.BlockSpec(memory_space=pltpu.SMEM), pl.BlockSpec(memory_space=pl.ANY)],
            out_specs=pl.BlockSpec(memory_space=pl.ANY),
            scratch_shapes=[
                pltpu.VMEM(pieces, survey.dtype),
                pltpu.VMEM((STEPS,) + pieces[2:], survey.dtype),
                pltpu.VMEM((tiles, 2, bins, height, tile), survey.dtype),
                pltpu.VMEM(column, survey.dtype),
                pltpu.VMEM(column, survey.dtype),
                pltpu.VMEM((bins, 2 * height, 6 * STEPS * PANEL), jnp.bfloat16),
                pltpu.VMEM(whole, survey.dtype),
                pltpu.SemaphoreType.DMA((tiles,)),
                pltpu.SemaphoreType.DMA((STEPS, tiles * bins)),
                pltpu.SemaphoreType.DMA((STEPS, SLOTS, WINDOW)),
                pltpu.SemaphoreType.DMA((STEPS,)),
                pltpu.SemaphoreType.DMA((STEPS,)),
                pltpu.SemaphoreType.DMA((STEPS, tiles * bins)),
                pltpu.SemaphoreType.DMA((2,)),
                pltpu.SemaphoreType.DMA,
            ],
            compiler_params=pltpu.CompilerParams(
                collective_id=number, has_side_effects=True, vmem_limit_bytes=48 << 20
            ),
            name="product_%d_%d" % pair,
        )

    pairs = [(i, j) for i in range(chips) for j in range(i, chips)]
    calls = [call(number, pair) for number, pair in enumerate(pairs)]
    number = pl.pallas_call(
        functools.partial(number_kernel, chips, 2 * height // PANEL),
        out_shape=jax.ShapeDtypeStruct((1,), jnp.int32),
        in_specs=[pl.BlockSpec(memory_space=pltpu.SMEM)],
        out_specs=pl.BlockSpec(memory_space=pltpu.SMEM),
        name="number",
    )(panel_index)
    freq = lax.switch(number[0], calls, panel_index, survey)
    return expand(freq)


def expand_kernel(freq_ref, table_ref, out_ref):
    samples, rows, tile = out_ref.shape
    nfreq = freq_ref.shape[1]
    half = samples // 2

    def group(g, carry):
        at = pl.ds(pl.multiple_of(8 * g, 8), 8)
        waves = []
        for i in (0, 1):
            part = freq_ref[0, :, i, at, :].reshape(8 * nfreq, tile)
            hi, lo = split(part)
            waves.append(dot(table_ref[i], jnp.concatenate([hi, lo, hi], axis=0)))
        even, odd = waves
        out_ref[half:, at, :] = (even - odd).reshape(half, 8, tile)
        early = even + odd
        for j in range(half):
            out_ref[half - 1 - j, at, :] = early[8 * j : 8 * j + 8]
        return carry

    lax.fori_loop(0, rows // 8, group, 0, unroll=2)


def expand(freq):
    tiles, bins, _, height, tile = freq.shape
    big = jnp.asarray(kron_tables(bins))
    return pl.pallas_call(
        expand_kernel,
        grid=(tiles,),
        out_shape=jax.ShapeDtypeStruct((SAMPLES, height, tiles * tile), jnp.float32),
        in_specs=[
            pl.BlockSpec((1,) + freq.shape[1:], lambda j: (j, 0, 0, 0, 0)),
            pl.BlockSpec(big.shape, lambda j: (0, 0, 0)),
        ],
        out_specs=pl.BlockSpec((SAMPLES, height, tile), lambda j: (0, 0, j)),
        compiler_params=pltpu.CompilerParams(vmem_limit_bytes=40 << 20),
        name="expand",
    )(freq, big)


def predict_kernel(
    own_ref, mine_ref, other_ref, row0_ref, row1_ref, table_ref, out_ref,
    left_hi, left_lo, freq_ref,
):
    nfreq = mine_ref.shape[1]
    rows = mine_ref.shape[2]
    tile = out_ref.shape[2]

    @pl.when(pl.program_id(0) == 0)
    def _():
        lane = lax.broadcasted_iota(jnp.int32, (rows, 2 * PANEL), 1)
        own = jnp.where(lane < PANEL, own_ref[0], own_ref[1]) == 1
        for f in range(nfreq):
            real = jnp.where(own, mine_ref[0, f], other_ref[0, f])
            imag = jnp.where(own, mine_ref[1, f], other_ref[1, f])
            cos, sin = middle(f)
            real, imag = real * cos - imag * sin, real * sin + imag * cos
            top = jnp.concatenate([real, -imag], axis=1)
            low = jnp.concatenate([imag, real], axis=1)
            hi, lo = split(jnp.concatenate([top, low], axis=0))
            left_hi[f] = hi
            left_lo[f] = lo

    for f in range(nfreq):
        right = jnp.concatenate(
            [row0_ref[0, f], row1_ref[0, f], row0_ref[1, f], row1_ref[1, f]], axis=0
        )
        hi, lo = split(right)
        both = dot(left_hi[f], hi) + dot(left_lo[f], hi) + dot(left_hi[f], lo)
        freq_ref[f] = both[:rows]
        freq_ref[nfreq + f] = both[rows:]

    half = SAMPLES // 2
    for g in range(rows // 8):
        at = slice(8 * g, 8 * g + 8)
        waves = []
        for i in (0, 1):
            part = freq_ref[i * nfreq : (i + 1) * nfreq, at, :].reshape(8 * nfreq, tile)
            hi, lo = split(part)
            waves.append(dot(table_ref[i], jnp.concatenate([hi, lo, hi], axis=0)))
        even, odd = waves
        out_ref[half:, at, :] = (even - odd).reshape(half, 8, tile)
        early = even + odd
        for j in range(half):
            out_ref[half - 1 - j, at, :] = early[8 * j : 8 * j + 8]


def predict(own, mine, other, row0, row1):
    _, nfreq, rows, width = mine.shape
    cols = row0.shape[3]
    tile = min(256, cols)
    big = jnp.asarray(kron_tables(nfreq))
    whole = pl.BlockSpec(mine.shape, lambda j: (0, 0, 0, 0))
    row_spec = pl.BlockSpec((2, nfreq, PANEL, tile), lambda j: (0, 0, 0, j))
    return pl.pallas_call(
        predict_kernel,
        grid=(cols // tile,),
        out_shape=jax.ShapeDtypeStruct((SAMPLES, rows, cols), jnp.float32),
        in_specs=[
            pl.BlockSpec(memory_space=pltpu.SMEM),
            whole,
            whole,
            row_spec,
            row_spec,
            pl.BlockSpec(big.shape, lambda j: (0, 0, 0)),
        ],
        out_specs=pl.BlockSpec((SAMPLES, rows, tile), lambda j: (0, 0, j)),
        scratch_shapes=[
            pltpu.VMEM((nfreq, 2 * rows, 4 * PANEL), jnp.bfloat16),
            pltpu.VMEM((nfreq, 2 * rows, 4 * PANEL), jnp.bfloat16),
            pltpu.VMEM((2 * nfreq, rows, tile), jnp.float32),
        ],
        compiler_params=pltpu.CompilerParams(vmem_limit_bytes=48 << 20),
        name="predict",
    )(own, mine, other, row0, row1, big)


def fetch_rows(source, start, shot_rows):
    length = min(shot_rows, PANEL)
    pieces = []
    for index_piece in range(PANEL // length):
        first = start + index_piece * length
        owner = first // shot_rows
        offset = first % shot_rows
        piece = lax.dynamic_slice_in_dim(source, offset, length, 2)
        pieces.append(from_root(piece, "shot", owner))
    return jnp.concatenate(pieces, axis=2)


def gathered(survey, panel_index):
    shot_rows = survey.shape[2]
    rec_cols = survey.shape[3]
    starts = [panel_index[step] * PANEL for step in range(STEPS)]
    columns = [
        lax.dynamic_slice_in_dim(survey, start % rec_cols, PANEL, 3) for start in starts
    ]
    owners = jnp.stack([start // rec_cols for start in starts])
    mine = jnp.concatenate(columns, axis=3)
    wanted = jnp.repeat(
        owners == lax.axis_index("rec"), PANEL, total_repeat_length=STEPS * PANEL
    )
    mine = lax.psum(jnp.where(wanted, mine, 0.0), "rec")
    own = jnp.ones((STEPS,), jnp.int32)
    rows = [fetch_rows(survey, start, shot_rows) for start in starts]
    return predict(own, mine, mine, rows[0], rows[1])


def solution(mesh):
    shots, recs = mesh.shape["shot"], mesh.shape["rec"]

    def shards(survey, panel_index):
        if (shots, recs) == (16, 2):
            return product(survey, panel_index, shots)
        return gathered(survey, panel_index)

    return jax.shard_map(
        shards,
        mesh=mesh,
        in_specs=(P(None, None, "shot", "rec"), P()),
        out_specs=P(None, "shot", "rec"),
        check_vma=False,
    )
```

```python
import functools
import math

import jax
import jax.numpy as jnp
import numpy as np
from jax import lax
from jax.experimental import pallas as pl
from jax.experimental.pallas import tpu as pltpu
from jax.sharding import PartitionSpec as P

FIRST_BIN = 8
TRACE_LEN = 400
SAMPLES = 64
PANEL = 64
STEPS = 2
SLOTS = 3
WINDOW = 4
LAG = 3
BEGIN = 24
RATE = 4
AHEAD = 4
FIELDS = (0, 2, 6, 7, 12, 17, 21, 25, 29)


def from_root(array, axis, root):
    mine = lax.axis_index(axis) == root
    return lax.psum(jnp.where(mine, array, jnp.zeros_like(array)), axis)


def middle(f):
    angle = 2.0 * math.pi * (f + FIRST_BIN) * (0.5 * (SAMPLES - 1)) / TRACE_LEN
    return math.cos(angle), math.sin(angle)


def kron_tables(nfreq):
    moments = np.arange(SAMPLES // 2) + 0.5
    bins = np.arange(nfreq) + FIRST_BIN
    angle = moments[:, None] * bins[None, :] * (2.0 * math.pi / TRACE_LEN)
    parts = []
    for wave in (np.cos(angle), np.sin(angle)):
        flat = np.kron(wave / math.sqrt(nfreq), np.eye(8)).astype(np.float32)
        hi = flat.astype(jnp.bfloat16)
        lo = (flat - hi.astype(np.float32)).astype(jnp.bfloat16)
        parts.append(np.concatenate([hi, hi, lo], axis=1))
    return np.stack(parts)


def tree(z0, y0, depth):
    last = depth - 1
    if z0 == 0:
        steps = [(0, 2), (2, 3), (2, 1)]
    elif z0 == last:
        steps = [(last, last - 2), (last - 2, last - 3), (last - 2, last - 1)]
    elif z0 == 1:
        steps = [(1, 2), (2, 3), (1, 0)]
    else:
        steps = [(2, 1), (1, 0), (2, 3)]
    back = z0 + 1 if z0 < last else z0 - 1
    halves = []
    for half in (0, 1):
        line = (y0 + half) % 2
        copies = [((z0, y0), (z0, line))] if half else []
        copies += [((z, line), (w, line)) for z, w in steps]
        copies += [((z, line), (z, 1 - line)) for z in range(depth) if z != z0]
        if half == 0:
            copies.append(((back, 1 - y0), (z0, 1 - y0)))
        halves.append(copies)
    return halves


def plan(chip, depth):
    owner = divmod(chip, 2)
    devices = 4 * depth
    targets = [[] for _ in range(devices)]
    parent = [-1] * devices
    hops = [0] * devices
    for half, copies in enumerate(tree(*owner, depth)):
        number = lambda at: 4 * at[0] + 2 * at[1] + half
        for source, target in copies:
            targets[number(source)].append(number(target))
            parent[number(target)] = number(source)
        for device in range(half, devices, 2):
            at = device
            while parent[at] >= 0:
                hops[device] += 1
                at = parent[at]
    return targets, parent, hops


def split(array):
    hi = array.astype(jnp.bfloat16)
    return hi, (array - hi.astype(jnp.float32)).astype(jnp.bfloat16)


def dot(left, right):
    return jnp.dot(left, right, preferred_element_type=jnp.float32)


def product_kernel(
    plans, panel_ref, survey_ref, out_ref,
    pan, swap, block, mine, other, left_all, freq,
    load_sem, recv_sem, send_sem, swap_sem, core_send, core_recv, side_sem, out_sem,
):
    me, rec = lax.axis_index("shot"), lax.axis_index("rec")
    c = me % 2
    peer = me + 1 - 2 * c
    tiles, _, bins, height, tile = block.shape
    count = tiles * bins
    low, high = panel_ref[0], panel_ref[1]
    panels = (jnp.minimum(low, high), jnp.maximum(low, high))

    depths = [hops for _, _, hops in plans]
    words, delays = [[], []], []
    for at in range(len(depths[0])):
        near = min(hops[at] for hops in depths)
        pair = (2 * (at // 2), 2 * (at // 2) + 1)
        delays.append(LAG * (max(hops[i] for hops in depths for i in pair) - near) + 2)
        for p, (targets, parents, hops) in enumerate(plans):
            fields = [len(targets[at]), max(parents[at], 0), int(parents[at] < 0), LAG * (hops[at] - near), delays[at]]
            fields += targets[at] + [0] * (SLOTS - len(targets[at]))
            words[p].append(sum(value << place for value, place in zip(fields, FIELDS)))

    def both_of(first, second):
        return lambda p: jnp.where(p == 0, first, second)

    word = []
    for p in range(STEPS):
        total = jnp.int32(0)
        for device, value in enumerate(words[p]):
            total = total + jnp.where(me == device, jnp.int32(value), jnp.int32(0))
        word.append(total)

    def field(at):
        width = FIELDS[at + 1] - FIELDS[at]
        parts = [lax.rem(lax.div(w, jnp.int32(1 << FIELDS[at])), jnp.int32(1 << width)) for w in word]
        return both_of(*parts)

    sends, parent, root, lag, delay = [field(at) for at in range(5)]
    targets = [field(5 + s) for s in range(SLOTS)]
    delay = delay(0)
    panel = both_of(*panels)

    def target(p, s):
        found = targets[0](p)
        for other_slot in range(1, SLOTS):
            found = jnp.where(s == other_slot, targets[other_slot](p), found)
        return found

    def each(count, body):
        def turn(at, carry):
            body(at)
            return carry

        lax.fori_loop(0, count, turn, 0)

    def load(j):
        return pltpu.make_async_copy(
            survey_ref.at[:, :, :, pl.ds(pl.multiple_of(j * tile, tile), tile)], block.at[j], load_sem.at[j]
        )

    each(tiles, lambda j: load(j).start())

    def remote(source, target, send, arrive, device):
        return pltpu.make_async_remote_copy(
            src_ref=source,
            dst_ref=target,
            send_sem=send,
            recv_sem=arrive,
            device_id=device,
            device_id_type=pl.DeviceIdType.MESH,
        )

    def exchange(p, k):
        to = pan.at[p, 1 - c, k]
        return remote(swap.at[p, k], to, swap_sem.at[p], recv_sem.at[p, k], {"shot": peer})

    def forward(p, s, k):
        piece = pan.at[p, c, k]
        send = send_sem.at[p, s, k % WINDOW]
        return remote(piece, piece, send, recv_sem.at[p, k], {"shot": target(p, s)})

    def share(p, half, k):
        piece = pan.at[p, half, k]
        return remote(piece, piece, core_send.at[p], core_recv.at[p, k], {"shot": peer})

    places = [panels[p] // 2 % (tiles * tile // (2 * PANEL)) for p in range(STEPS)]
    odd = [panels[p] % 2 for p in range(STEPS)]

    def rows(p, half, k):
        j, f = k // bins, k % bins
        first, second = block[j, half, f, :PANEL, :], block[j, half, f, PANEL:, :]
        return jnp.where(panel(p) % 2 == 0, first, second)

    def offer(p, k):
        swap[p, k] = rows(p, 1 - c, k)
        exchange(p, k).start()

    def side(at):
        return remote(mine.at[at], other.at[at], side_sem.at[0], side_sem.at[1], {"rec": 1 - rec})

    def columns(at):
        lane = lax.broadcasted_iota(jnp.int32, (height, 2 * PANEL), 1)
        i, f = at // bins, at % bins

        def look(j, parts):
            for first in range(0, tile, 2 * PANEL):
                place = j * (tile // (2 * PANEL)) + first // (2 * PANEL)
                whole = block[j, i, f, :, first : first + 2 * PANEL]
                parts = [jnp.where(places[p] == place, whole, parts[p]) for p in range(STEPS)]
            return parts

        nothing = jnp.zeros((height, 2 * PANEL), jnp.float32)
        parts = lax.fori_loop(0, tiles, look, [nothing] * STEPS)
        for p in range(STEPS):
            parts[p] = jnp.where(odd[p] == p, parts[p], pltpu.roll(parts[p], PANEL, 1))
        mine[at] = jnp.where(lane < PANEL, parts[0], parts[1])
        side(at).start()

    def left(f):
        part = height // 2
        lane = lax.broadcasted_iota(jnp.int32, (part, 2 * PANEL), 1)
        place = jnp.where(lane < PANEL, panels[0], panels[1])
        own = place * PANEL // (tiles * tile) == rec
        cos, sin = jnp.float32(0), jnp.float32(0)
        for g in range(bins):
            cos = jnp.where(f == g, jnp.float32(middle(g)[0]), cos)
            sin = jnp.where(f == g, jnp.float32(middle(g)[1]), sin)

        def body(at):
            at = pl.multiple_of(at * part, part)
            line = pl.ds(at, part)
            real = jnp.where(own, mine[f, line], other[f, line])
            imag = jnp.where(own, mine[bins + f, line], other[bins + f, line])
            first, second = real * cos - imag * sin, real * sin + imag * cos
            for start, pair in ((0, [first, -second]), (height, [second, first])):
                hi, lo = split(jnp.concatenate(pair, axis=1))
                left_all[f, pl.ds(start + at, part)] = jnp.concatenate([hi, lo, hi], axis=1)

        each(2, body)

    def multiply(k):
        j, f = k // bins, k % bins
        whole = jnp.concatenate([pan[0, 0, k], pan[1, 0, k], pan[0, 1, k], pan[1, 1, k]], axis=0)
        hi, lo = split(whole)
        both = dot(left_all[f], jnp.concatenate([hi, hi, lo], axis=0))
        freq[j, f, 0] = both[:height]
        freq[j, f, 1] = both[height:]
        pltpu.make_async_copy(freq.at[j, f], out_ref.at[j, f], out_sem).start()

    barrier = pltpu.get_barrier_semaphore()

    def enter(device):
        pl.semaphore_signal(barrier, inc=1, device_id=device, device_id_type=pl.DeviceIdType.MESH)

    def greet(p):
        @pl.when(root(p) == 0)
        def _():
            enter({"shot": parent(p)})

    each(STEPS, greet)
    enter({"shot": peer})
    enter({"rec": 1 - rec})
    pl.semaphore_wait(barrier, sends(0) + sends(1) + 2)

    load(0).wait()

    def done(t):
        return jnp.maximum(jnp.minimum(jnp.minimum(RATE * (t - BEGIN), t - delay), count), 0)

    def pass_on(p, k):
        piece = pan.at[p, c, k]
        remote(piece, piece, core_send.at[p], recv_sem.at[p, k], {"shot": peer}).wait_recv()

        @pl.when(root(p) == 1)
        def _():
            ours = panel(p) // 2 % 2 == c
            pan[p, c, k] = jnp.where(ours, rows(p, c, k), pan[p, c, k])

        def send(s):
            @pl.when(k >= WINDOW)
            def _():
                forward(p, s, k - WINDOW).wait_send()

            forward(p, s, k).start()

        each(sends(p), send)
        share(p, c, k).start()

    def step(t):
        def turn(p):
            k = t - lag(p)

            @pl.when((root(p) == 1) & (k < count - AHEAD))
            def _():
                offer(p, k + AHEAD)

            @pl.when((k >= 0) & (k < count))
            def _():
                pass_on(p, k)

        each(STEPS, turn)

        @pl.when(t == 0)
        def _():
            each(tiles - 1, lambda j: load(j + 1).wait())

        @pl.when((t >= 1) & (t <= bins))
        def _():
            each(2, lambda at: columns(2 * t - 2 + at))

        @pl.when(t == BEGIN - bins // 2)
        def _():
            remote(mine, other, side_sem.at[0], side_sem.at[1], {"rec": 1 - rec}).wait_recv()

        @pl.when((t >= BEGIN - bins // 2) & (t < BEGIN))
        def _():
            each(2, lambda at: left(2 * (t - BEGIN) + bins + at))

        def product_of(k, carry):
            for p in range(STEPS):
                share(p, 1 - c, k).wait_recv()
            multiply(k)
            return carry

        lax.fori_loop(done(t), done(t + 1), product_of, 0)

    each(AHEAD + max(count + max(delays), BEGIN + count // RATE), lambda at: step(at - AHEAD))

    def finish(p):
        def drain(s):
            each(WINDOW, lambda at: forward(p, s, count - WINDOW + at).wait_send())

        each(sends(p), drain)
        remote(pan.at[p, c], pan.at[p, c], core_send.at[p], recv_sem.at[p, 0], {"shot": peer}).wait_send()

        @pl.when(root(p) == 1)
        def _():
            to = pan.at[p, 1 - c]
            remote(swap.at[p], to, swap_sem.at[p], recv_sem.at[p, 0], {"shot": peer}).wait_send()

    each(STEPS, finish)
    remote(mine, other, side_sem.at[0], side_sem.at[1], {"rec": 1 - rec}).wait_send()
    pltpu.make_async_copy(freq, out_ref, out_sem).wait()


def number_kernel(chips, each, panel_ref, out_ref):
    first, second = panel_ref[0], panel_ref[1]
    i = jnp.minimum(first, second) // each
    j = jnp.maximum(first, second) // each
    out_ref[0] = i * chips - i * (i + 1) // 2 + j


def product(survey, panel_index, shots):
    _, bins, height, width = survey.shape
    tile = min(256, width)
    tiles = width // tile
    depth = shots // 4
    chips = shots // 2
    pieces = (STEPS, 2, tiles * bins, PANEL, tile)
    whole = (tiles, bins, 2, height, tile)
    column = (2 * bins, height, STEPS * PANEL)

    def call(number, pair):
        plans = [plan(chip, depth) for chip in pair]
        return pl.pallas_call(
            functools.partial(product_kernel, plans),
            out_shape=jax.ShapeDtypeStruct(whole, survey.dtype),
            in_specs=[pl.BlockSpec(memory_space=pltpu.SMEM), pl.BlockSpec(memory_space=pl.ANY)],
            out_specs=pl.BlockSpec(memory_space=pl.ANY),
            scratch_shapes=[
                pltpu.VMEM(pieces, survey.dtype),
                pltpu.VMEM((STEPS,) + pieces[2:], survey.dtype),
                pltpu.VMEM((tiles, 2, bins, height, tile), survey.dtype),
                pltpu.VMEM(column, survey.dtype),
                pltpu.VMEM(column, survey.dtype),
                pltpu.VMEM((bins, 2 * height, 6 * STEPS * PANEL), jnp.bfloat16),
                pltpu.VMEM(whole, survey.dtype),
                pltpu.SemaphoreType.DMA((tiles,)),
                pltpu.SemaphoreType.DMA((STEPS, tiles * bins)),
                pltpu.SemaphoreType.DMA((STEPS, SLOTS, WINDOW)),
                pltpu.SemaphoreType.DMA((STEPS,)),
                pltpu.SemaphoreType.DMA((STEPS,)),
                pltpu.SemaphoreType.DMA((STEPS, tiles * bins)),
                pltpu.SemaphoreType.DMA((2,)),
                pltpu.SemaphoreType.DMA,
            ],
            compiler_params=pltpu.CompilerParams(
                collective_id=number, has_side_effects=True, vmem_limit_bytes=48 << 20
            ),
            name="product_%d_%d" % pair,
        )

    pairs = [(i, j) for i in range(chips) for j in range(i, chips)]
    calls = [call(number, pair) for number, pair in enumerate(pairs)]
    number = pl.pallas_call(
        functools.partial(number_kernel, chips, 2 * height // PANEL),
        out_shape=jax.ShapeDtypeStruct((1,), jnp.int32),
        in_specs=[pl.BlockSpec(memory_space=pltpu.SMEM)],
        out_specs=pl.BlockSpec(memory_space=pltpu.SMEM),
        name="number",
    )(panel_index)
    freq = lax.switch(number[0], calls, panel_index, survey)
    return expand(freq)


def expand_kernel(freq_ref, table_ref, out_ref):
    samples, rows, tile = out_ref.shape
    nfreq = freq_ref.shape[1]
    half = samples // 2

    def group(g, carry):
        at = pl.ds(pl.multiple_of(8 * g, 8), 8)
        waves = []
        for i in (0, 1):
            part = freq_ref[0, :, i, at, :].reshape(8 * nfreq, tile)
            hi, lo = split(part)
            waves.append(dot(table_ref[i], jnp.concatenate([hi, lo, hi], axis=0)))
        even, odd = waves
        out_ref[half:, at, :] = (even - odd).reshape(half, 8, tile)
        early = even + odd
        for j in range(half):
            out_ref[half - 1 - j, at, :] = early[8 * j : 8 * j + 8]
        return carry

    lax.fori_loop(0, rows // 8, group, 0, unroll=8)


def expand(freq):
    tiles, bins, _, height, tile = freq.shape
    big = jnp.asarray(kron_tables(bins))
    return pl.pallas_call(
        expand_kernel,
        grid=(tiles,),
        out_shape=jax.ShapeDtypeStruct((SAMPLES, height, tiles * tile), jnp.float32),
        in_specs=[
            pl.BlockSpec((1,) + freq.shape[1:], lambda j: (j, 0, 0, 0, 0)),
            pl.BlockSpec(big.shape, lambda j: (0, 0, 0)),
        ],
        out_specs=pl.BlockSpec((SAMPLES, height, tile), lambda j: (0, 0, j)),
        compiler_params=pltpu.CompilerParams(vmem_limit_bytes=40 << 20),
        name="expand",
    )(freq, big)


def predict_kernel(
    own_ref, mine_ref, other_ref, row0_ref, row1_ref, table_ref, out_ref,
    left_hi, left_lo, freq_ref,
):
    nfreq = mine_ref.shape[1]
    rows = mine_ref.shape[2]
    tile = out_ref.shape[2]

    @pl.when(pl.program_id(0) == 0)
    def _():
        lane = lax.broadcasted_iota(jnp.int32, (rows, 2 * PANEL), 1)
        own = jnp.where(lane < PANEL, own_ref[0], own_ref[1]) == 1
        for f in range(nfreq):
            real = jnp.where(own, mine_ref[0, f], other_ref[0, f])
            imag = jnp.where(own, mine_ref[1, f], other_ref[1, f])
            cos, sin = middle(f)
            real, imag = real * cos - imag * sin, real * sin + imag * cos
            top = jnp.concatenate([real, -imag], axis=1)
            low = jnp.concatenate([imag, real], axis=1)
            hi, lo = split(jnp.concatenate([top, low], axis=0))
            left_hi[f] = hi
            left_lo[f] = lo

    for f in range(nfreq):
        right = jnp.concatenate(
            [row0_ref[0, f], row1_ref[0, f], row0_ref[1, f], row1_ref[1, f]], axis=0
        )
        hi, lo = split(right)
        both = dot(left_hi[f], hi) + dot(left_lo[f], hi) + dot(left_hi[f], lo)
        freq_ref[f] = both[:rows]
        freq_ref[nfreq + f] = both[rows:]

    half = SAMPLES // 2
    for g in range(rows // 8):
        at = slice(8 * g, 8 * g + 8)
        waves = []
        for i in (0, 1):
            part = freq_ref[i * nfreq : (i + 1) * nfreq, at, :].reshape(8 * nfreq, tile)
            hi, lo = split(part)
            waves.append(dot(table_ref[i], jnp.concatenate([hi, lo, hi], axis=0)))
        even, odd = waves
        out_ref[half:, at, :] = (even - odd).reshape(half, 8, tile)
        early = even + odd
        for j in range(half):
            out_ref[half - 1 - j, at, :] = early[8 * j : 8 * j + 8]


def predict(own, mine, other, row0, row1):
    _, nfreq, rows, width = mine.shape
    cols = row0.shape[3]
    tile = min(256, cols)
    big = jnp.asarray(kron_tables(nfreq))
    whole = pl.BlockSpec(mine.shape, lambda j: (0, 0, 0, 0))
    row_spec = pl.BlockSpec((2, nfreq, PANEL, tile), lambda j: (0, 0, 0, j))
    return pl.pallas_call(
        predict_kernel,
        grid=(cols // tile,),
        out_shape=jax.ShapeDtypeStruct((SAMPLES, rows, cols), jnp.float32),
        in_specs=[
            pl.BlockSpec(memory_space=pltpu.SMEM),
            whole,
            whole,
            row_spec,
            row_spec,
            pl.BlockSpec(big.shape, lambda j: (0, 0, 0)),
        ],
        out_specs=pl.BlockSpec((SAMPLES, rows, tile), lambda j: (0, 0, j)),
        scratch_shapes=[
            pltpu.VMEM((nfreq, 2 * rows, 4 * PANEL), jnp.bfloat16),
            pltpu.VMEM((nfreq, 2 * rows, 4 * PANEL), jnp.bfloat16),
            pltpu.VMEM((2 * nfreq, rows, tile), jnp.float32),
        ],
        compiler_params=pltpu.CompilerParams(vmem_limit_bytes=48 << 20),
        name="predict",
    )(own, mine, other, row0, row1, big)


def fetch_rows(source, start, shot_rows):
    length = min(shot_rows, PANEL)
    pieces = []
    for index_piece in range(PANEL // length):
        first = start + index_piece * length
        owner = first // shot_rows
        offset = first % shot_rows
        piece = lax.dynamic_slice_in_dim(source, offset, length, 2)
        pieces.append(from_root(piece, "shot", owner))
    return jnp.concatenate(pieces, axis=2)


def gathered(survey, panel_index):
    shot_rows = survey.shape[2]
    rec_cols = survey.shape[3]
    starts = [panel_index[step] * PANEL for step in range(STEPS)]
    columns = [
        lax.dynamic_slice_in_dim(survey, start % rec_cols, PANEL, 3) for start in starts
    ]
    owners = jnp.stack([start // rec_cols for start in starts])
    mine = jnp.concatenate(columns, axis=3)
    wanted = jnp.repeat(
        owners == lax.axis_index("rec"), PANEL, total_repeat_length=STEPS * PANEL
    )
    mine = lax.psum(jnp.where(wanted, mine, 0.0), "rec")
    own = jnp.ones((STEPS,), jnp.int32)
    rows = [fetch_rows(survey, start, shot_rows) for start in starts]
    return predict(own, mine, mine, rows[0], rows[1])


def solution(mesh):
    shots, recs = mesh.shape["shot"], mesh.shape["rec"]

    def shards(survey, panel_index):
        if (shots, recs) == (16, 2):
            return product(survey, panel_index, shots)
        return gathered(survey, panel_index)

    return jax.shard_map(
        shards,
        mesh=mesh,
        in_specs=(P(None, None, "shot", "rec"), P()),
        out_specs=P(None, "shot", "rec"),
        check_vma=False,
    )
```
